32 devices in a mesh: expert: 4 (over y, core), dp: 2 (over x), tensor: 4 (over z).
Axes of the slice: x: 2, y: 2, z: 4, core: 2. Of those that a mesh axis runs over, the one named last changes fastest.
Arguments:
- tokens: bfloat16 [128, 4096], P(('expert', 'dp')), may hold values from -6 to 6
- expert_ids: int32 [128, 2], P(('expert', 'dp')), may hold values from 0 to 3, all different within a row; in each aligned block of 16 rows (0 to 15, 16 to 31, ...) at most 12 rows name the same one
- route_weight: float32 [128, 2], P(('expert', 'dp')), may hold values from 0.2 to 1
- gate_weight: bfloat16 [4, 4096, 8192], P('expert', None, ('dp', 'tensor')), may hold values from -0.09375 to 0.09375
- up_weight: bfloat16 [4, 4096, 8192], P('expert', None, ('dp', 'tensor')), may hold values from -0.09375 to 0.09375
- down_weight: bfloat16 [4, 8192, 4096], P('expert', 'dp', 'tensor'), may hold values from -0.125 to 0.125
- past_layers: bfloat16 [8, 128, 4096], P(None, ('expert', 'dp'), 'tensor'), may hold values from -6 to 6
- dwa_weight: float32 [9], replicated, may hold values from 0.3 to 1.2
Outputs:
- mixed: bfloat16 [128, 4096], P(('expert', 'dp'), 'tensor')
The draws below stay inside these ranges and needn't reach their ends.
Inputs may be any that keep to these rules, and one draw needn't show every extreme that they name: `expert_ids`: each row names 2 different experts. In each aligned block of 16 rows (the rows of one device) no expert is named more than 12 times; in some blocks one expert is named exactly 12 times.
All inputs are finite; a program needn't handle non-finite values.
Results may differ from the reference program's by a relative error of at most 0.009.
Values may be sent and summed in bfloat16 or wider, within the bound.
A program may use at most 64 MiB of HBM per device.

```python
import math
import jax
import jax.numpy as jnp
import numpy as np
from jax import lax

D = 4096
FF = 8192
TOP = 2
PAST = 8
TOK_DEV = 16
EXPERTS = 4
CAP = 12
TOKENS = 128


def levels(key, shape, split, smallest, high):
    def one(axis_at, shards_of):
        steps = jax.random.uniform(jax.random.fold_in(jax.random.fold_in(key, 6), axis_at), (shards_of,), jnp.float32, smallest / len(split), high / len(split))
        return jnp.repeat(jnp.exp(steps), shape[axis_at] // shards_of).reshape((-1,) + (1,) * (len(shape) - axis_at - 1))

    gain = one(*split[0])
    for cut in split[1:]:
        gain = gain * one(*cut)
    return gain


def assign_block(key, own, number, rows, count, top, most, slope):
    ranking = jax.random.permutation(key, count)
    packed, usual = load_shares(count, rows * top, most, slope, True), load_shares(count, rows * top, most, slope, False)
    places = jnp.arange(count)

    def named(tallies, offset_by):
        used = int((tallies > 0).sum())
        fixed = max(1, used // 4)
        shifted = fixed + (places - fixed + offset_by * (used - fixed)) % max(1, count - fixed)
        return jnp.zeros((count,), jnp.int32).at[ranking[jnp.where(places < fixed, places, shifted)]].set(jnp.asarray(tallies, jnp.int32))

    tallies = jnp.where(number % 4 == 0, named(packed, number // 4), named(usual, number - number // 4 - 1))
    mixed = jax.random.permutation(jax.random.fold_in(own, 3), count)
    giver, receiver = mixed[0:count // 2 * 2:2], mixed[1:count // 2 * 2:2]
    margin = jnp.minimum(tallies[giver] - 1, most - tallies[receiver]) // 2
    margin = jnp.where((giver == ranking[0]) | (receiver == ranking[0]) | (tallies[receiver] == 0), 0, jnp.maximum(margin, 0))
    shifted = jax.random.randint(jax.random.fold_in(own, 4), (count // 2,), 0, 1 << 20) % (margin + 1)
    tallies = tallies.at[giver].add(-shifted).at[receiver].add(shifted)
    items = jnp.searchsorted(jnp.cumsum(tallies), jnp.arange(rows * top), side="right").astype(jnp.int32)
    listing = items.reshape(top, rows).T
    listing = listing[jax.random.permutation(jax.random.fold_in(own, 1), rows)]
    offset_by = jax.random.randint(jax.random.fold_in(own, 2), (rows, 1), 0, top)
    return jnp.take_along_axis(listing, (jnp.arange(top)[None, :] + offset_by) % top, axis=1)


def load_shares(amount, total, limit, skew, full):
    loads = [(1 << 20) // math.isqrt(rank ** skew) + 1 for rank in range(1, amount + 1)]
    largest = limit if full else min(limit, max(-(-total // amount), total * loads[0] // sum(loads)))
    least = 1 if total - largest >= amount - 1 else 0
    counts, surplus = [largest] + [least] * (amount - 1), total - largest - least * (amount - 1)
    while surplus > 0:
        movable = [i for i in range(1, amount) if counts[i] < largest] or [i for i in range(1, amount) if counts[i] < limit]
        whole, budget = sum([loads[i] for i in movable]), surplus
        for i in movable:
            extra = min(limit - counts[i], max(1, budget * loads[i] // whole), surplus)
            counts[i] = counts[i] + extra
            surplus = surplus - extra
    return np.array(counts)


def bell_draw(own_key, dims, spread, limit, cuts=(), kind=jnp.bfloat16):
    array = jax.random.normal(own_key, dims, jnp.float32) * spread
    if len(cuts) > 0:
        array = levels(own_key, dims, cuts, -0.22, 0.18) * array
    return jnp.clip(array, min=-limit, max=limit).astype(kind)


def setup_inputs(seed: int = 0) -> dict:
    splits = jax.random.split(jax.random.key(seed), 9)
    tokens = bell_draw(splits[0], (TOKENS, D), 1.0, 6.0, ((0, 8),))
    expert_ids_keys = jax.random.split(jax.random.fold_in(splits[1], 1), TOKENS // TOK_DEV)
    expert_ids_turns = jax.random.permutation(jax.random.fold_in(splits[1], 3), TOKENS // TOK_DEV)
    expert_ids = jax.vmap(lambda own, number: assign_block(jax.random.fold_in(splits[1], 2), own, number, TOK_DEV, EXPERTS, TOP, CAP, 2))(expert_ids_keys, expert_ids_turns).reshape((TOKENS, TOP))
    route_weight = jnp.clip(0.2 + 0.8 * jax.random.uniform(splits[2], (TOKENS, TOP), jnp.float32) ** levels(splits[2], (TOKENS, TOP), ((0, 8),), -0.2, 0.2), 0.2, 1.0)
    gate_weight = bell_draw(splits[3], (EXPERTS, D, FF), D ** -0.5, 0.09375, ((0, 4), (2, 8)))
    up_weight = bell_draw(splits[4], (EXPERTS, D, FF), D ** -0.5, 0.09375, ((0, 4), (2, 8)))
    down_weight = bell_draw(splits[5], (EXPERTS, FF, D), (FF // 4) ** -0.5, 0.125, ((0, 4), (1, 2), (2, 4)))
    past_layers = bell_draw(splits[6], (PAST, TOKENS, D), 1.0, 6.0, ((1, 8), (2, 4)))
    dwa_weight = jnp.clip(jax.random.uniform(splits[7], (PAST + 1,), jnp.float32, 0.3, 1.2), 0.3, 1.2)
    return dict(tokens=tokens, expert_ids=expert_ids, route_weight=route_weight, gate_weight=gate_weight, up_weight=up_weight, down_weight=down_weight, past_layers=past_layers, dwa_weight=dwa_weight)


def expert_slots(expert_ids):
    shards = TOKENS // TOK_DEV
    flat_ids = expert_ids.reshape(shards, TOK_DEV * TOP).astype(jnp.int32)
    matches = (flat_ids[:, :, None] == jnp.arange(EXPERTS, dtype=jnp.int32)[None, None, :]).astype(jnp.int32)
    earlier = jnp.cumsum(matches, axis=1) - matches
    slot_ids = jnp.sum(earlier * matches, axis=2).astype(jnp.int32)
    positions = jnp.arange(shards, dtype=jnp.int32)[:, None] * CAP + slot_ids
    return flat_ids, positions


def reference(tokens, expert_ids, route_weight, gate_weight, up_weight, down_weight, past_layers, dwa_weight):
    shards = TOKENS // TOK_DEV
    buffer_rows = shards * CAP
    flat_ids, positions = expert_slots(expert_ids)
    sources = jnp.repeat(jnp.arange(TOKENS, dtype=jnp.int32).reshape(shards, TOK_DEV), TOP, axis=1)

    def run_expert(inputs):
        number, w_gate, w_up, w_down = inputs
        targets = jnp.where(flat_ids == number, positions, buffer_rows).reshape(-1).astype(jnp.int32)
        picked = jnp.zeros((buffer_rows + 1,), jnp.int32).at[targets].set(sources.reshape(-1))
        rows = tokens[picked[:buffer_rows]]
        gate = jnp.dot(rows, w_gate, preferred_element_type=jnp.float32)
        up = jnp.dot(rows, w_up, preferred_element_type=jnp.float32)
        hidden = (jax.nn.silu(gate) * up).astype(jnp.bfloat16)
        return jnp.dot(hidden, w_down, preferred_element_type=jnp.float32).astype(jnp.bfloat16)

    outputs = lax.map(run_expert, (jnp.arange(EXPERTS, dtype=jnp.int32), gate_weight, up_weight, down_weight))
    index = (flat_ids * buffer_rows + positions).reshape(-1).astype(jnp.int32)
    fetched = outputs.reshape(EXPERTS * buffer_rows, D)[index].astype(jnp.float32).reshape(TOKENS, TOP, D)
    shares = route_weight / jnp.sum(route_weight, axis=1, keepdims=True)
    current = tokens.astype(jnp.float32) + jnp.sum(fetched * shares[:, :, None], axis=1)
    history = jnp.einsum("j,jtd->td", dwa_weight[:PAST].astype(jnp.float32), past_layers.astype(jnp.float32))
    return (dwa_weight[PAST] * current + history).astype(jnp.bfloat16)
```

```python
import functools

import jax
import jax.numpy as jnp
from jax import lax
from jax.experimental import pallas as pl
from jax.experimental.pallas import tpu as pltpu
from jax.sharding import PartitionSpec as P

MESH = pl.DeviceIdType.MESH
F32 = jnp.float32
BF16 = jnp.bfloat16


def arrival_order(n):
    table = []
    for z in range(n):
        order = [z]
        for k in range(1, n):
            order += [o for o in (z - k, z + k) if 0 <= o < n]
        table.append(order)
    return table


def kernel(
    sizes,
    tokens,
    ids,
    route,
    w_gate,
    w_up,
    w_down,
    past,
    dwa,
    out,
    rows_in,
    gate_buf,
    up_buf,
    down_buf,
    past_buf,
    hidden,
    acc,
    outgoing,
    incoming,
    base,
    local_sem,
    gate_sem,
    up_sem,
    down_sem,
    past_sem,
    tok_send,
    pair_send,
    tok_recv,
    z_send,
    z_recv,
    mix_send,
    mix_recv,
):
    n_exp, n_dp, n_ten, pieces, tok_rows, quarter = sizes
    columns = n_exp // 2
    in_group = 2 * n_dp
    e, d, z = (lax.axis_index(a) for a in ("expert", "dp", "tensor"))
    core = lax.rem(e, 2)
    col = lax.div(e, 2)
    partner = e + 1 - 2 * core
    piece = gate_buf.shape[2]

    def rows_at(position):
        return pl.ds(pl.multiple_of(position * tok_rows, tok_rows), tok_rows)

    loads = []
    own_place = core * n_dp + d
    own_load = pltpu.make_async_copy(tokens, rows_in.at[0, rows_at(own_place)], local_sem)
    own_load.start()
    for s in range(pieces):
        part = pl.ds(s * piece, piece)
        loads.append(
            (
                pltpu.make_async_copy(w_gate.at[0, :, part], gate_buf.at[s], gate_sem.at[s]),
                pltpu.make_async_copy(w_up.at[0, :, part], up_buf.at[s], up_sem.at[s]),
            )
        )
        for copy in loads[-1]:
            copy.start()
    past_load = pltpu.make_async_copy(past, past_buf, past_sem)
    past_load.start()
    table = arrival_order(n_ten)
    order = []
    for j in range(n_ten):
        o = jnp.int32(0)
        for i in range(n_ten):
            o = o + jnp.where(z == i, table[i][j], 0)
        order.append(o)
    depth = n_ten and down_buf.shape[1]
    down_loads = []
    for j in range(n_ten):
        o = order[j]
        down_loads.append(
            pltpu.make_async_copy(
                w_down.at[0, pl.ds(pl.multiple_of(o * depth, depth), depth)],
                down_buf.at[o],
                down_sem.at[o],
            )
        )
        down_loads[-1].start()

    barrier = pltpu.get_barrier_semaphore()
    peers = [(i, j) for i in range(n_exp) for j in range(n_dp) if (i, j) != (0, 0)]
    for i, j in peers:
        pl.semaphore_signal(
            barrier,
            inc=1,
            device_id=(lax.rem(e + i, n_exp), lax.rem(d + j, n_dp), z),
            device_id_type=MESH,
        )
    has_up = z < n_ten - 1
    has_down = z > 0
    if n_ten > 1:

        @pl.when(has_up)
        def _():
            pl.semaphore_signal(barrier, inc=1, device_id=(e, d, z + 1), device_id_type=MESH)

        @pl.when(has_down)
        def _():
            pl.semaphore_signal(barrier, inc=1, device_id=(e, d, z - 1), device_id_type=MESH)

    pl.semaphore_wait(barrier, len(peers) + has_up.astype(jnp.int32) + has_down.astype(jnp.int32))

    def to_partner(g, place, slot):
        source = tokens if slot == (0, 0) else rows_in.at[g, rows_at(place)]
        return pltpu.make_async_remote_copy(
            source,
            rows_in.at[g, rows_at(place)],
            pair_send.at[slot[0], slot[1]],
            tok_recv.at[g, place],
            device_id=(partner, d, z),
            device_id_type=MESH,
        )

    def direct(g, dd):
        return pltpu.make_async_remote_copy(
            tokens,
            rows_in.at[g, rows_at(own_place)],
            tok_send.at[g, dd],
            tok_recv.at[g, own_place],
            device_id=(
                2 * lax.rem(col + columns - g, columns) + core,
                lax.rem(d + dd, n_dp),
                z,
            ),
            device_id_type=MESH,
        )

    sends = [to_partner(0, own_place, (0, 0))]
    sends[0].start()
    hops = [(g, dd) for g in range(columns) for dd in range(n_dp) if (g, dd) != (0, 0)]
    for g, dd in sorted(hops, key=lambda h: (h[0] > 0) + (h[1] > 0)):
        copy = direct(g, dd)
        copy.start()
        sends.append(copy)

    def wait_tokens(g, place):
        pltpu.make_async_remote_copy(
            tokens,
            rows_in.at[g, rows_at(place)],
            tok_send.at[0, 0],
            tok_recv.at[g, place],
            device_id=(partner, d, z),
            device_id_type=MESH,
        ).wait_recv()

    def pass_on(g):
        for dd in range(n_dp):
            if (g, dd) == (0, 0):
                continue
            place = core * n_dp + lax.rem(d + n_dp - dd, n_dp)
            wait_tokens(g, place)
            copy = to_partner(g, place, (g, dd))
            copy.start()
            sends.append(copy)

    def from_partner(g):
        for dd in range(n_dp):
            wait_tokens(g, (1 - core) * n_dp + dd)

    def hop(g, o, s, up):
        return pltpu.make_async_remote_copy(
            hidden.at[g, o, s],
            hidden.at[g, o, s],
            z_send.at[g, o, s, 0 if up else 1],
            z_recv.at[g, o, s],
            device_id=(e, d, z + 1 if up else z - 1),
            device_id_type=MESH,
        )

    def first_half(g):
        for s in range(pieces):
            if g == 0:
                for copy in loads[s]:
                    copy.wait()
            rows = rows_in[g]
            gate = jnp.dot(rows, gate_buf[s], preferred_element_type=F32)
            up = jnp.dot(rows, up_buf[s], preferred_element_type=F32)
            hidden[g, z, s] = (gate / (1.0 + jnp.exp(-gate)) * up).astype(BF16)

            @pl.when(has_up)
            def _():
                hop(g, z, s, True).start()

            @pl.when(has_down)
            def _():
                hop(g, z, s, False).start()

    def relay(g, j):
        o = order[j]
        for s in range(pieces):
            hop(g, o, s, True).wait_recv()

            @pl.when((o < z) & has_up)
            def _():
                hop(g, o, s, True).start()

            @pl.when((o > z) & has_down)
            def _():
                hop(g, o, s, False).start()

    def second_half(g, j):
        o = order[j]
        total = None
        for s in range(pieces):
            term = jnp.dot(
                hidden[g, o, s],
                down_buf[o, pl.ds(s * piece, piece), :],
                preferred_element_type=F32,
            )
            total = term if total is None else total + term
        if j == 0:
            acc[g] = total
        else:
            acc[g] += total

    me = e * n_dp + d

    def give(g):
        outgoing[g] = acc[g].astype(BF16)
        copies = []
        for k in range(2):
            for dd in range(n_dp):
                place = lax.rem(core + k, 2) * n_dp + lax.rem(d + dd, n_dp)
                if (g, k, dd) == (0, 0, 0):
                    incoming[me] = outgoing[g, rows_at(place), :]
                    continue
                copy = pltpu.make_async_remote_copy(
                    outgoing.at[g, rows_at(place)],
                    incoming.at[me],
                    mix_send.at[g, k, dd],
                    mix_recv.at[me],
                    device_id=(
                        2 * lax.rem(col + g, columns) + lax.rem(core + k, 2),
                        lax.rem(d + dd, n_dp),
                        z,
                    ),
                    device_id_type=MESH,
                )
                copy.start()
                copies.append(copy)
        return copies

    past_load.wait()
    layers = past_buf.shape[0]
    history = dwa[0] * past_buf[0].astype(F32)
    for j in range(1, layers):
        history = history + dwa[j] * past_buf[j].astype(F32)
    base[...] = history
    own_load.wait()
    pass_on(0)
    from_partner(0)
    first_half(0)
    residual = rows_in[0, rows_at(own_place), pl.ds(pl.multiple_of(z * quarter, quarter), quarter)]
    base[...] += dwa[layers] * residual.astype(F32)
    for g in range(1, columns):
        pass_on(g)
        from_partner(g)
        first_half(g)
    mixes = []
    for j in range(n_ten):
        for g in range(columns):
            if j > 0:
                relay(g, j)
            if g == 0:
                down_loads[j].wait()
            second_half(g, j)
            if j == n_ten - 1:
                mixes += give(g)

    shares = route[...] / jnp.sum(route[...], axis=1, keepdims=True)
    total = base[...]
    mixed = jnp.zeros_like(total)
    for i in range(n_exp):
        weight = jnp.sum(jnp.where(ids[...] == i, shares, 0.0), axis=1, keepdims=True)
        both = None
        for j in range(n_dp):
            source = i * n_dp + j

            @pl.when(source != me)
            def _():
                pltpu.make_async_remote_copy(
                    incoming.at[source],
                    incoming.at[source],
                    mix_send.at[0, 0, 0],
                    mix_recv.at[source],
                    device_id=(partner, d, z),
                    device_id_type=MESH,
                ).wait_recv()

            term = incoming[source].astype(F32)
            both = term if both is None else both + term
        mixed = mixed + weight * both
    out[...] = (total + dwa[layers] * mixed).astype(BF16)

    for copy in sends + mixes:
        copy.wait_send()
    for g in range(columns):
        for s in range(pieces):
            for o in range(n_ten):

                @pl.when((o <= z) & has_up)
                def _():
                    hop(g, o, s, True).wait_send()

                @pl.when((o >= z) & has_down)
                def _():
                    hop(g, o, s, False).wait_send()


def solution(mesh):
    n_exp, n_dp, n_ten = (mesh.shape[a] for a in ("expert", "dp", "tensor"))

    def per_device(tokens, ids, route, w_gate, w_up, w_down, past, dwa):
        tok_rows, width = tokens.shape
        units = w_gate.shape[2]
        quarter = w_down.shape[2]
        pieces = 2 if units % 512 == 0 else 1
        piece = units // pieces
        columns, group_rows = n_exp // 2, 2 * n_dp * tok_rows
        blocks = n_exp * n_dp
        any_spec = pl.BlockSpec(memory_space=pl.ANY)
        vmem = pl.BlockSpec(memory_space=pltpu.VMEM)
        smem = pl.BlockSpec(memory_space=pltpu.SMEM)
        dma = pltpu.SemaphoreType.DMA
        return pl.pallas_call(
            functools.partial(kernel, (n_exp, n_dp, n_ten, pieces, tok_rows, quarter)),
            out_shape=jax.ShapeDtypeStruct((tok_rows, quarter), BF16),
            in_specs=[any_spec, vmem, vmem, any_spec, any_spec, any_spec, any_spec, smem],
            out_specs=vmem,
            scratch_shapes=[
                pltpu.VMEM((columns, group_rows, width), BF16),
                pltpu.VMEM((pieces, width, piece), BF16),
                pltpu.VMEM((pieces, width, piece), BF16),
                pltpu.VMEM((n_ten, units, quarter), BF16),
                pltpu.VMEM(past.shape, BF16),
                pltpu.VMEM((columns, n_ten, pieces, group_rows, piece), BF16),
                pltpu.VMEM((columns, group_rows, quarter), F32),
                pltpu.VMEM((columns, group_rows, quarter), BF16),
                pltpu.VMEM((blocks, tok_rows, quarter), BF16),
                pltpu.VMEM((tok_rows, quarter), F32),
                dma,
                dma((pieces,)),
                dma((pieces,)),
                dma((n_ten,)),
                dma,
                dma((columns, n_dp)),
                dma((columns, n_dp)),
                dma((columns, 2 * n_dp)),
                dma((columns, n_ten, pieces, 2)),
                dma((columns, n_ten, pieces)),
                dma((columns, 2, n_dp)),
                dma((blocks,)),
            ],
            compiler_params=pltpu.CompilerParams(
                collective_id=0, has_side_effects=True, vmem_limit_bytes=60 * 1024 * 1024
            ),
        )(tokens, ids, route, w_gate, w_up, w_down, past, dwa)

    return jax.shard_map(
        per_device,
        mesh=mesh,
        in_specs=(
            P(("expert", "dp"), None),
            P(("expert", "dp"), None),
            P(("expert", "dp"), None),
            P("expert", None, ("dp", "tensor")),
            P("expert", None, ("dp", "tensor")),
            P("expert", "dp", "tensor"),
            P(None, ("expert", "dp"), "tensor"),
            P(),
        ),
        out_specs=P(("expert", "dp"), "tensor"),
        check_vma=False,
    )
```

```python
import functools

import jax
import jax.numpy as jnp
from jax import lax
from jax.experimental import pallas as pl
from jax.experimental.pallas import tpu as pltpu
from jax.sharding import PartitionSpec as P

MESH = pl.DeviceIdType.MESH
F32 = jnp.float32
BF16 = jnp.bfloat16


def arrival_order(n):
    table = []
    for z in range(n):
        order = [z]
        for k in range(1, n):
            order += [o for o in (z - k, z + k) if 0 <= o < n]
        table.append(order)
    return table


def kernel(
    sizes,
    tokens,
    ids,
    route,
    w_gate,
    w_up,
    w_down,
    past,
    dwa,
    out,
    rows_in,
    gate_buf,
    up_buf,
    down_buf,
    past_buf,
    hidden,
    acc,
    outgoing,
    incoming,
    base,
    mark,
    marks,
    pick,
    place_back,
    local_sem,
    gate_sem,
    up_sem,
    down_sem,
    past_sem,
    tok_send,
    pair_send,
    tok_recv,
    z_send,
    z_recv,
    mix_send,
    mix_recv,
    mark_send,
    mark_recv,
):
    n_exp, n_dp, n_ten, pieces, tok_rows, quarter, capacity = sizes
    columns = n_exp // 2
    in_group = 2 * n_dp
    e, d, z = (lax.axis_index(a) for a in ("expert", "dp", "tensor"))
    core = lax.rem(e, 2)
    col = lax.div(e, 2)
    partner = e + 1 - 2 * core
    piece = gate_buf.shape[2]

    def rows_at(position):
        return pl.ds(pl.multiple_of(position * tok_rows, tok_rows), tok_rows)

    loads = []
    own_place = core * n_dp + d
    own_load = pltpu.make_async_copy(tokens, rows_in.at[0, rows_at(own_place)], local_sem)
    own_load.start()
    for s in range(pieces):
        part = pl.ds(s * piece, piece)
        loads.append(
            (
                pltpu.make_async_copy(w_gate.at[0, :, part], gate_buf.at[s], gate_sem.at[s]),
                pltpu.make_async_copy(w_up.at[0, :, part], up_buf.at[s], up_sem.at[s]),
            )
        )
    past_load = pltpu.make_async_copy(past, past_buf, past_sem)
    past_load.start()
    table = arrival_order(n_ten)
    order = []
    for j in range(n_ten):
        o = jnp.int32(0)
        for i in range(n_ten):
            o = o + jnp.where(z == i, table[i][j], 0)
        order.append(o)
    depth = down_buf.shape[1]
    down_loads = []
    for j in range(n_ten):
        o = order[j]
        down_loads.append(
            pltpu.make_async_copy(
                w_down.at[0, pl.ds(pl.multiple_of(o * depth, depth), depth)],
                down_buf.at[o],
                down_sem.at[o],
            )
        )

    group_rows = in_group * tok_rows
    expert_row = lax.broadcasted_iota(jnp.int32, (mark.shape[0], tok_rows), 0)
    named = jnp.zeros(expert_row.shape, F32)
    for k in range(ids.shape[0]):
        named = named + jnp.where(ids[k : k + 1, :] == expert_row, 1.0, 0.0)
    token_at = lax.broadcasted_iota(jnp.int32, (tok_rows, group_rows), 0) + own_place * tok_rows
    spot = jnp.where(lax.broadcasted_iota(jnp.int32, token_at.shape, 1) == token_at, 1.0, 0.0)
    mark[...] = jnp.dot(named, spot, preferred_element_type=F32)

    barrier = pltpu.get_barrier_semaphore()
    peers = [(i, j) for i in range(n_exp) for j in range(n_dp) if (i, j) != (0, 0)]
    for i, j in peers:
        pl.semaphore_signal(
            barrier,
            inc=1,
            device_id=(lax.rem(e + i, n_exp), lax.rem(d + j, n_dp), z),
            device_id_type=MESH,
        )
    has_up = z < n_ten - 1
    has_down = z > 0
    if n_ten > 1:

        @pl.when(has_up)
        def _():
            pl.semaphore_signal(barrier, inc=1, device_id=(e, d, z + 1), device_id_type=MESH)

        @pl.when(has_down)
        def _():
            pl.semaphore_signal(barrier, inc=1, device_id=(e, d, z - 1), device_id_type=MESH)

    pl.semaphore_wait(barrier, len(peers) + has_up.astype(jnp.int32) + has_down.astype(jnp.int32))

    def to_partner(g, place, slot):
        source = tokens if slot == (0, 0) else rows_in.at[g, rows_at(place)]
        return pltpu.make_async_remote_copy(
            source,
            rows_in.at[g, rows_at(place)],
            pair_send.at[slot[0], slot[1]],
            tok_recv.at[g, place],
            device_id=(partner, d, z),
            device_id_type=MESH,
        )

    def direct(g, dd):
        return pltpu.make_async_remote_copy(
            tokens,
            rows_in.at[g, rows_at(own_place)],
            tok_send.at[g, dd],
            tok_recv.at[g, own_place],
            device_id=(
                2 * lax.rem(col + columns - g, columns) + core,
                lax.rem(d + dd, n_dp),
                z,
            ),
            device_id_type=MESH,
        )

    me = e * n_dp + d
    marks[me] = mark[...]
    sends = []
    for i, j in peers:
        copy = pltpu.make_async_remote_copy(
            mark,
            marks.at[me],
            mark_send.at[i, j],
            mark_recv.at[me],
            device_id=(lax.rem(e + i, n_exp), lax.rem(d + j, n_dp), z),
            device_id_type=MESH,
        )
        copy.start()
        sends.append(copy)
    sends.append(to_partner(0, own_place, (0, 0)))
    sends[-1].start()
    hops = [(g, dd) for g in range(columns) for dd in range(n_dp) if (g, dd) != (0, 0)]
    for g, dd in sorted(hops, key=lambda h: (h[0] > 0) + (h[1] > 0)):
        copy = direct(g, dd)
        copy.start()
        sends.append(copy)

    for pair in loads:
        for copy in pair:
            copy.start()
    for copy in down_loads:
        copy.start()

    def wait_tokens(g, place):
        pltpu.make_async_remote_copy(
            tokens,
            rows_in.at[g, rows_at(place)],
            tok_send.at[0, 0],
            tok_recv.at[g, place],
            device_id=(partner, d, z),
            device_id_type=MESH,
        ).wait_recv()

    def pass_on(g):
        for dd in range(n_dp):
            if (g, dd) == (0, 0):
                continue
            place = core * n_dp + lax.rem(d + n_dp - dd, n_dp)
            wait_tokens(g, place)
            copy = to_partner(g, place, (g, dd))
            copy.start()
            sends.append(copy)

    def from_partner(g):
        for dd in range(n_dp):
            wait_tokens(g, (1 - core) * n_dp + dd)

    def hop(g, o, s, up):
        return pltpu.make_async_remote_copy(
            hidden.at[g, o, s],
            hidden.at[g, o, s],
            z_send.at[g, o, s, 0 if up else 1],
            z_recv.at[g, o, s],
            device_id=(e, d, z + 1 if up else z - 1),
            device_id_type=MESH,
        )

    def choose(g):
        total = jnp.zeros(mark.shape, F32)
        for c in range(2):
            for dd in range(n_dp):
                source = (2 * lax.rem(col + columns - g, columns) + c) * n_dp + dd

                @pl.when(source != me)
                def _():
                    pltpu.make_async_remote_copy(
                        mark,
                        marks.at[source],
                        mark_send.at[0, 1],
                        mark_recv.at[source],
                        device_id=(partner, d, z),
                        device_id_type=MESH,
                    ).wait_recv()

                total = total + marks[source]
        square = (group_rows, group_rows)
        before = lax.broadcasted_iota(jnp.int32, square, 0)
        after = lax.broadcasted_iota(jnp.int32, square, 1)
        block = lax.div(after, tok_rows)
        earlier = (before < after) & (lax.div(before, tok_rows) == block)
        slot = jnp.dot(total, jnp.where(earlier, 1.0, 0.0), preferred_element_type=F32)
        lane_block = lax.div(lax.broadcasted_iota(jnp.int32, mark.shape, 1), tok_rows)
        target = jnp.where(total > 0.5, slot + (lane_block * capacity).astype(F32), -1.0)
        mine = lax.broadcasted_iota(jnp.int32, mark.shape, 0) == e
        row = jnp.sum(jnp.where(mine, target, 0.0), axis=0, keepdims=True)
        column = jnp.sum(jnp.where(before == after, row, 0.0), axis=1, keepdims=True)
        down_slots = lax.broadcasted_iota(jnp.int32, pick.shape[1:], 0).astype(F32)
        across = lax.broadcasted_iota(jnp.int32, place_back.shape[1:], 1).astype(F32)
        pick[g] = jnp.where(down_slots == row, 1.0, 0.0).astype(BF16)
        place_back[g] = jnp.where(across == column, 1.0, 0.0).astype(BF16)

    def first_half(g):
        for s in range(pieces):
            if g == 0:
                for copy in loads[s]:
                    copy.wait()
            rows = rows_in[g]
            gate = jnp.dot(rows, gate_buf[s], preferred_element_type=F32)
            up = jnp.dot(rows, up_buf[s], preferred_element_type=F32)
            value = (gate / (1.0 + jnp.exp(-gate)) * up).astype(BF16)
            hidden[g, z, s] = jnp.dot(pick[g], value, preferred_element_type=F32).astype(BF16)

            @pl.when(has_up)
            def _():
                hop(g, z, s, True).start()

            @pl.when(has_down)
            def _():
                hop(g, z, s, False).start()

    def relay(g, j):
        o = order[j]
        for s in range(pieces):
            hop(g, o, s, True).wait_recv()

            @pl.when((o < z) & has_up)
            def _():
                hop(g, o, s, True).start()

            @pl.when((o > z) & has_down)
            def _():
                hop(g, o, s, False).start()

    def second_half(g, j):
        o = order[j]
        total = None
        for s in range(pieces):
            term = jnp.dot(
                hidden[g, o, s],
                down_buf[o, pl.ds(s * piece, piece), :],
                preferred_element_type=F32,
            )
            total = term if total is None else total + term
        if j == 0:
            acc[g] = total
        else:
            acc[g] += total

    def give(g):
        outgoing[g] = jnp.dot(
            place_back[g], acc[g].astype(BF16), preferred_element_type=F32
        ).astype(BF16)
        copies = []
        for k in range(2):
            for dd in range(n_dp):
                place = lax.rem(core + k, 2) * n_dp + lax.rem(d + dd, n_dp)
                if (g, k, dd) == (0, 0, 0):
                    incoming[me] = outgoing[g, rows_at(place), :]
                    continue
                copy = pltpu.make_async_remote_copy(
                    outgoing.at[g, rows_at(place)],
                    incoming.at[me],
                    mix_send.at[g, k, dd],
                    mix_recv.at[me],
                    device_id=(
                        2 * lax.rem(col + g, columns) + lax.rem(core + k, 2),
                        lax.rem(d + dd, n_dp),
                        z,
                    ),
                    device_id_type=MESH,
                )
                copy.start()
                copies.append(copy)
        return copies

    past_load.wait()
    layers = past_buf.shape[0]
    history = dwa[0] * past_buf[0].astype(F32)
    for j in range(1, layers):
        history = history + dwa[j] * past_buf[j].astype(F32)
    base[...] = history
    own_load.wait()
    choose(0)
    pass_on(0)
    from_partner(0)
    first_half(0)
    residual = rows_in[0, rows_at(own_place), pl.ds(pl.multiple_of(z * quarter, quarter), quarter)]
    base[...] += dwa[layers] * residual.astype(F32)
    for g in range(1, columns):
        choose(g)
        pass_on(g)
        from_partner(g)
        first_half(g)
    mixes = []
    for j in range(n_ten):
        for g in range(columns):
            if j > 0:
                relay(g, j)
            if g == 0:
                down_loads[j].wait()
            second_half(g, j)
            if j == n_ten - 1:
                mixes += give(g)

    shares = route[...] / jnp.sum(route[...], axis=0, keepdims=True)
    corner = (tok_rows, tok_rows)
    diagonal = lax.broadcasted_iota(jnp.int32, corner, 0) == lax.broadcasted_iota(jnp.int32, corner, 1)
    total = base[...]
    mixed = jnp.zeros_like(total)
    for i in range(n_exp):
        weight = jnp.sum(jnp.where(ids[...] == i, shares, 0.0), axis=0, keepdims=True)
        weight = jnp.sum(jnp.where(diagonal, weight, 0.0), axis=1, keepdims=True)
        both = None
        for j in range(n_dp):
            source = i * n_dp + j

            @pl.when(source != me)
            def _():
                pltpu.make_async_remote_copy(
                    incoming.at[source],
                    incoming.at[source],
                    mix_send.at[0, 0, 0],
                    mix_recv.at[source],
                    device_id=(partner, d, z),
                    device_id_type=MESH,
                ).wait_recv()

            term = incoming[source].astype(F32)
            both = term if both is None else both + term
        mixed = mixed + weight * both
    out[...] = (total + dwa[layers] * mixed).astype(BF16)

    for copy in sends + mixes:
        copy.wait_send()
    for g in range(columns):
        for s in range(pieces):
            for o in range(n_ten):

                @pl.when((o <= z) & has_up)
                def _():
                    hop(g, o, s, True).wait_send()

                @pl.when((o >= z) & has_down)
                def _():
                    hop(g, o, s, False).wait_send()


def solution(mesh):
    n_exp, n_dp, n_ten = (mesh.shape[a] for a in ("expert", "dp", "tensor"))

    def per_device(tokens, ids, route, w_gate, w_up, w_down, past, dwa):
        tok_rows, width = tokens.shape
        units = w_gate.shape[2]
        quarter = w_down.shape[2]
        pieces = 2 if units % 512 == 0 else 1
        piece = units // pieces
        columns, group_rows = n_exp // 2, 2 * n_dp * tok_rows
        capacity = min(tok_rows, 3 * ids.shape[1] * tok_rows // (2 * n_exp))
        packed = 2 * n_dp * capacity
        named = 8 * pl.cdiv(n_exp, 8)
        blocks = n_exp * n_dp
        any_spec = pl.BlockSpec(memory_space=pl.ANY)
        vmem = pl.BlockSpec(memory_space=pltpu.VMEM)
        smem = pl.BlockSpec(memory_space=pltpu.SMEM)
        dma = pltpu.SemaphoreType.DMA
        return pl.pallas_call(
            functools.partial(kernel, (n_exp, n_dp, n_ten, pieces, tok_rows, quarter, capacity)),
            out_shape=jax.ShapeDtypeStruct((tok_rows, quarter), BF16),
            in_specs=[any_spec, vmem, vmem, any_spec, any_spec, any_spec, any_spec, smem],
            out_specs=vmem,
            scratch_shapes=[
                pltpu.VMEM((columns, group_rows, width), BF16),
                pltpu.VMEM((pieces, width, piece), BF16),
                pltpu.VMEM((pieces, width, piece), BF16),
                pltpu.VMEM((n_ten, units, quarter), BF16),
                pltpu.VMEM(past.shape, BF16),
                pltpu.VMEM((columns, n_ten, pieces, packed, piece), BF16),
                pltpu.VMEM((columns, packed, quarter), F32),
                pltpu.VMEM((columns, group_rows, quarter), BF16),
                pltpu.VMEM((blocks, tok_rows, quarter), BF16),
                pltpu.VMEM((tok_rows, quarter), F32),
                pltpu.VMEM((named, group_rows), F32),
                pltpu.VMEM((blocks, named, group_rows), F32),
                pltpu.VMEM((columns, packed, group_rows), BF16),
                pltpu.VMEM((columns, group_rows, packed), BF16),
                dma,
                dma((pieces,)),
                dma((pieces,)),
                dma((n_ten,)),
                dma,
                dma((columns, n_dp)),
                dma((columns, n_dp)),
                dma((columns, 2 * n_dp)),
                dma((columns, n_ten, pieces, 2)),
                dma((columns, n_ten, pieces)),
                dma((columns, 2, n_dp)),
                dma((blocks,)),
                dma((n_exp, n_dp)),
                dma((blocks,)),
            ],
            compiler_params=pltpu.CompilerParams(
                collective_id=0, has_side_effects=True, vmem_limit_bytes=60 * 1024 * 1024
            ),
        )(tokens, ids.T, route.T, w_gate, w_up, w_down, past, dwa)

    return jax.shard_map(
        per_device,
        mesh=mesh,
        in_specs=(
            P(("expert", "dp"), None),
            P(("expert", "dp"), None),
            P(("expert", "dp"), None),
            P("expert", None, ("dp", "tensor")),
            P("expert", None, ("dp", "tensor")),
            P("expert", "dp", "tensor"),
            P(None, ("expert", "dp"), "tensor"),
            P(),
        ),
        out_specs=P(("expert", "dp"), "tensor"),
        check_vma=False,
    )
```

```python
import functools

import jax
import jax.numpy as jnp
from jax import lax
from jax.experimental import pallas as pl
from jax.experimental.pallas import tpu as pltpu
from jax.sharding import PartitionSpec as P

MESH = pl.DeviceIdType.MESH
F32 = jnp.float32
BF16 = jnp.bfloat16


def arrival_order(n):
    table = []
    for z in range(n):
        order = [z]
        for k in range(1, n):
            order += [o for o in (z - k, z + k) if 0 <= o < n]
        table.append(order)
    return table


def kernel(
    sizes,
    tokens,
    ids,
    route,
    w_gate,
    w_up,
    w_down,
    past,
    dwa,
    out,
    rows_in,
    gate_buf,
    up_buf,
    down_buf,
    past_buf,
    hidden,
    acc,
    outgoing,
    incoming,
    base,
    mark,
    marks,
    pick,
    place_back,
    local_sem,
    gate_sem,
    up_sem,
    down_sem,
    past_sem,
    tok_send,
    pair_send,
    tok_recv,
    z_send,
    z_recv,
    mix_send,
    mix_recv,
    mark_send,
    mark_recv,
):
    n_exp, n_dp, n_ten, pieces, tok_rows, quarter, capacity = sizes
    columns = n_exp // 2
    in_group = 2 * n_dp
    e, d, z = (lax.axis_index(a) for a in ("expert", "dp", "tensor"))
    core = lax.rem(e, 2)
    col = lax.div(e, 2)
    partner = e + 1 - 2 * core
    piece = gate_buf.shape[2]

    def rows_at(position):
        return pl.ds(pl.multiple_of(position * tok_rows, tok_rows), tok_rows)

    loads = []
    own_place = core * n_dp + d
    own_load = pltpu.make_async_copy(tokens, rows_in.at[0, rows_at(own_place)], local_sem)
    own_load.start()
    for s in range(pieces):
        part = pl.ds(s * piece, piece)
        loads.append(
            (
                pltpu.make_async_copy(w_gate.at[0, :, part], gate_buf.at[s], gate_sem.at[s]),
                pltpu.make_async_copy(w_up.at[0, :, part], up_buf.at[s], up_sem.at[s]),
            )
        )
    past_load = pltpu.make_async_copy(past, past_buf, past_sem)
    past_load.start()
    table = arrival_order(n_ten)
    order = []
    for j in range(n_ten):
        o = jnp.int32(0)
        for i in range(n_ten):
            o = o + jnp.where(z == i, table[i][j], 0)
        order.append(o)
    depth = down_buf.shape[1]
    down_loads = []
    for j in range(n_ten):
        o = order[j]
        down_loads.append(
            pltpu.make_async_copy(
                w_down.at[0, pl.ds(pl.multiple_of(o * depth, depth), depth)],
                down_buf.at[o],
                down_sem.at[o],
            )
        )

    group_rows = in_group * tok_rows
    expert_row = lax.broadcasted_iota(jnp.int32, (mark.shape[0], tok_rows), 0)
    named = jnp.zeros(expert_row.shape, F32)
    for k in range(ids.shape[0]):
        named = named + jnp.where(ids[k : k + 1, :] == expert_row, 1.0, 0.0)
    token_at = lax.broadcasted_iota(jnp.int32, (tok_rows, group_rows), 0) + own_place * tok_rows
    spot = jnp.where(lax.broadcasted_iota(jnp.int32, token_at.shape, 1) == token_at, 1.0, 0.0)
    mark[...] = jnp.dot(named, spot, preferred_element_type=F32)

    barrier = pltpu.get_barrier_semaphore()
    peers = [(i, j) for i in range(n_exp) for j in range(n_dp) if (i, j) != (0, 0)]
    for i, j in peers:
        pl.semaphore_signal(
            barrier,
            inc=1,
            device_id=(lax.rem(e + i, n_exp), lax.rem(d + j, n_dp), z),
            device_id_type=MESH,
        )
    has_up = z < n_ten - 1
    has_down = z > 0
    if n_ten > 1:

        @pl.when(has_up)
        def _():
            pl.semaphore_signal(barrier, inc=1, device_id=(e, d, z + 1), device_id_type=MESH)

        @pl.when(has_down)
        def _():
            pl.semaphore_signal(barrier, inc=1, device_id=(e, d, z - 1), device_id_type=MESH)

    pl.semaphore_wait(barrier, len(peers) + has_up.astype(jnp.int32) + has_down.astype(jnp.int32))

    def to_partner(g, place, slot):
        source = tokens if slot == (0, 0) else rows_in.at[g, rows_at(place)]
        return pltpu.make_async_remote_copy(
            source,
            rows_in.at[g, rows_at(place)],
            pair_send.at[slot[0], slot[1]],
            tok_recv.at[g, place],
            device_id=(partner, d, z),
            device_id_type=MESH,
        )

    def direct(g, dd):
        return pltpu.make_async_remote_copy(
            tokens,
            rows_in.at[g, rows_at(own_place)],
            tok_send.at[g, dd],
            tok_recv.at[g, own_place],
            device_id=(
                2 * lax.rem(col + columns - g, columns) + core,
                lax.rem(d + dd, n_dp),
                z,
            ),
            device_id_type=MESH,
        )

    me = e * n_dp + d
    marks[me] = mark[...]
    sends = []
    for i, j in peers:
        copy = pltpu.make_async_remote_copy(
            mark,
            marks.at[me],
            mark_send.at[i, j],
            mark_recv.at[me],
            device_id=(lax.rem(e + i, n_exp), lax.rem(d + j, n_dp), z),
            device_id_type=MESH,
        )
        copy.start()
        sends.append(copy)
    sends.append(to_partner(0, own_place, (0, 0)))
    sends[-1].start()
    hops = [(g, dd) for g in range(columns) for dd in range(n_dp) if (g, dd) != (0, 0)]
    for g, dd in sorted(hops, key=lambda h: (h[0] > 0) + (h[1] > 0)):
        copy = direct(g, dd)
        copy.start()
        sends.append(copy)

    for pair in loads:
        for copy in pair:
            copy.start()
    for copy in down_loads:
        copy.start()

    def wait_tokens(g, place):
        pltpu.make_async_remote_copy(
            tokens,
            rows_in.at[g, rows_at(place)],
            tok_send.at[0, 0],
            tok_recv.at[g, place],
            device_id=(partner, d, z),
            device_id_type=MESH,
        ).wait_recv()

    def pass_on(g, steps):
        for dd in steps:
            if (g, dd) == (0, 0):
                continue
            place = core * n_dp + lax.rem(d + n_dp - dd, n_dp)
            wait_tokens(g, place)
            copy = to_partner(g, place, (g, dd))
            copy.start()
            sends.append(copy)

    def from_partner(g):
        for dd in range(n_dp):
            wait_tokens(g, (1 - core) * n_dp + dd)

    def hop(g, o, s, up):
        return pltpu.make_async_remote_copy(
            hidden.at[g, o, s],
            hidden.at[g, o, s],
            z_send.at[g, o, s, 0 if up else 1],
            z_recv.at[g, o, s],
            device_id=(e, d, z + 1 if up else z - 1),
            device_id_type=MESH,
        )

    def choose(g):
        total = jnp.zeros(mark.shape, F32)
        for c in range(2):
            for dd in range(n_dp):
                source = (2 * lax.rem(col + columns - g, columns) + c) * n_dp + dd

                @pl.when(source != me)
                def _():
                    pltpu.make_async_remote_copy(
                        mark,
                        marks.at[source],
                        mark_send.at[0, 1],
                        mark_recv.at[source],
                        device_id=(partner, d, z),
                        device_id_type=MESH,
                    ).wait_recv()

                total = total + marks[source]
        square = (group_rows, group_rows)
        before = lax.broadcasted_iota(jnp.int32, square, 0)
        after = lax.broadcasted_iota(jnp.int32, square, 1)
        block = lax.div(after, tok_rows)
        earlier = (before < after) & (lax.div(before, tok_rows) == block)
        slot = jnp.dot(total, jnp.where(earlier, 1.0, 0.0), preferred_element_type=F32)
        lane_block = lax.div(lax.broadcasted_iota(jnp.int32, mark.shape, 1), tok_rows)
        target = jnp.where(total > 0.5, slot + (lane_block * capacity).astype(F32), -1.0)
        mine = lax.broadcasted_iota(jnp.int32, mark.shape, 0) == e
        row = jnp.sum(jnp.where(mine, target, 0.0), axis=0, keepdims=True)
        column = jnp.sum(jnp.where(before == after, row, 0.0), axis=1, keepdims=True)
        down_slots = lax.broadcasted_iota(jnp.int32, pick.shape[1:], 0).astype(F32)
        across = lax.broadcasted_iota(jnp.int32, place_back.shape[1:], 1).astype(F32)
        pick[g] = jnp.where(down_slots == row, 1.0, 0.0).astype(BF16)
        place_back[g] = jnp.where(across == column, 1.0, 0.0).astype(BF16)

    def first_half(g):
        for s in range(pieces):
            if g == 0:
                for copy in loads[s]:
                    copy.wait()
            rows = rows_in[g]
            gate = jnp.dot(rows, gate_buf[s], preferred_element_type=F32)
            up = jnp.dot(rows, up_buf[s], preferred_element_type=F32)
            value = (gate / (1.0 + jnp.exp(-gate)) * up).astype(BF16)
            hidden[g, z, s] = jnp.dot(pick[g], value, preferred_element_type=F32).astype(BF16)

            @pl.when(has_up)
            def _():
                hop(g, z, s, True).start()

            @pl.when(has_down)
            def _():
                hop(g, z, s, False).start()

    def relay(g, j):
        o = order[j]
        for s in range(pieces):
            hop(g, o, s, True).wait_recv()

            @pl.when((o < z) & has_up)
            def _():
                hop(g, o, s, True).start()

            @pl.when((o > z) & has_down)
            def _():
                hop(g, o, s, False).start()

    def second_half(g, j):
        o = order[j]
        total = None
        for s in range(pieces):
            term = jnp.dot(
                hidden[g, o, s],
                down_buf[o, pl.ds(s * piece, piece), :],
                preferred_element_type=F32,
            )
            total = term if total is None else total + term
        if j == 0:
            acc[g] = total
        else:
            acc[g] += total

    def give(g):
        outgoing[g] = jnp.dot(
            place_back[g], acc[g].astype(BF16), preferred_element_type=F32
        ).astype(BF16)
        copies = []
        for k in range(2):
            for dd in range(n_dp):
                place = lax.rem(core + k, 2) * n_dp + lax.rem(d + dd, n_dp)
                if (g, k, dd) == (0, 0, 0):
                    incoming[me] = outgoing[g, rows_at(place), :]
                    continue
                copy = pltpu.make_async_remote_copy(
                    outgoing.at[g, rows_at(place)],
                    incoming.at[me],
                    mix_send.at[g, k, dd],
                    mix_recv.at[me],
                    device_id=(
                        2 * lax.rem(col + g, columns) + lax.rem(core + k, 2),
                        lax.rem(d + dd, n_dp),
                        z,
                    ),
                    device_id_type=MESH,
                )
                copy.start()
                copies.append(copy)
        return copies

    own_load.wait()
    choose(0)
    pass_on(0, range(n_dp))
    for g in range(1, columns):
        pass_on(g, range(1))
    from_partner(0)
    first_half(0)
    residual = rows_in[0, rows_at(own_place), pl.ds(pl.multiple_of(z * quarter, quarter), quarter)]
    past_load.wait()
    layers = past_buf.shape[0]
    history = dwa[0] * past_buf[0].astype(F32)
    for j in range(1, layers):
        history = history + dwa[j] * past_buf[j].astype(F32)
    base[...] = history
    base[...] += dwa[layers] * residual.astype(F32)
    for g in range(1, columns):
        choose(g)
        pass_on(g, range(1, n_dp))
        from_partner(g)
        first_half(g)
    mixes = []
    for j in range(n_ten):
        for g in range(columns):
            if j > 0:
                relay(g, j)
            if g == 0:
                down_loads[j].wait()
            second_half(g, j)
            if j == n_ten - 1:
                mixes += give(g)

    shares = route[...] / jnp.sum(route[...], axis=0, keepdims=True)
    corner = (tok_rows, tok_rows)
    diagonal = lax.broadcasted_iota(jnp.int32, corner, 0) == lax.broadcasted_iota(jnp.int32, corner, 1)
    total = base[...]
    mixed = jnp.zeros_like(total)
    for i in range(n_exp):
        weight = jnp.sum(jnp.where(ids[...] == i, shares, 0.0), axis=0, keepdims=True)
        weight = jnp.sum(jnp.where(diagonal, weight, 0.0), axis=1, keepdims=True)
        both = None
        for j in range(n_dp):
            source = i * n_dp + j

            @pl.when(source != me)
            def _():
                pltpu.make_async_remote_copy(
                    incoming.at[source],
                    incoming.at[source],
                    mix_send.at[0, 0, 0],
                    mix_recv.at[source],
                    device_id=(partner, d, z),
                    device_id_type=MESH,
                ).wait_recv()

            term = incoming[source].astype(F32)
            both = term if both is None else both + term
        mixed = mixed + weight * both
    out[...] = (total + dwa[layers] * mixed).astype(BF16)

    for copy in sends + mixes:
        copy.wait_send()
    for g in range(columns):
        for s in range(pieces):
            for o in range(n_ten):

                @pl.when((o <= z) & has_up)
                def _():
                    hop(g, o, s, True).wait_send()

                @pl.when((o >= z) & has_down)
                def _():
                    hop(g, o, s, False).wait_send()


def solution(mesh):
    n_exp, n_dp, n_ten = (mesh.shape[a] for a in ("expert", "dp", "tensor"))

    def per_device(tokens, ids, route, w_gate, w_up, w_down, past, dwa):
        tok_rows, width = tokens.shape
        units = w_gate.shape[2]
        quarter = w_down.shape[2]
        pieces = 2 if units % 512 == 0 else 1
        piece = units // pieces
        columns, group_rows = n_exp // 2, 2 * n_dp * tok_rows
        capacity = min(tok_rows, 3 * ids.shape[1] * tok_rows // (2 * n_exp))
        packed = 2 * n_dp * capacity
        named = 8 * pl.cdiv(n_exp, 8)
        blocks = n_exp * n_dp
        any_spec = pl.BlockSpec(memory_space=pl.ANY)
        vmem = pl.BlockSpec(memory_space=pltpu.VMEM)
        smem = pl.BlockSpec(memory_space=pltpu.SMEM)
        dma = pltpu.SemaphoreType.DMA
        return pl.pallas_call(
            functools.partial(kernel, (n_exp, n_dp, n_ten, pieces, tok_rows, quarter, capacity)),
            out_shape=jax.ShapeDtypeStruct((tok_rows, quarter), BF16),
            in_specs=[any_spec, vmem, vmem, any_spec, any_spec, any_spec, any_spec, smem],
            out_specs=vmem,
            scratch_shapes=[
                pltpu.VMEM((columns, group_rows, width), BF16),
                pltpu.VMEM((pieces, width, piece), BF16),
                pltpu.VMEM((pieces, width, piece), BF16),
                pltpu.VMEM((n_ten, units, quarter), BF16),
                pltpu.VMEM(past.shape, BF16),
                pltpu.VMEM((columns, n_ten, pieces, packed, piece), BF16),
                pltpu.VMEM((columns, packed, quarter), F32),
                pltpu.VMEM((columns, group_rows, quarter), BF16),
                pltpu.VMEM((blocks, tok_rows, quarter), BF16),
                pltpu.VMEM((tok_rows, quarter), F32),
                pltpu.VMEM((named, group_rows), F32),
                pltpu.VMEM((blocks, named, group_rows), F32),
                pltpu.VMEM((columns, packed, group_rows), BF16),
                pltpu.VMEM((columns, group_rows, packed), BF16),
                dma,
                dma((pieces,)),
                dma((pieces,)),
                dma((n_ten,)),
                dma,
                dma((columns, n_dp)),
                dma((columns, n_dp)),
                dma((columns, 2 * n_dp)),
                dma((columns, n_ten, pieces, 2)),
                dma((columns, n_ten, pieces)),
                dma((columns, 2, n_dp)),
                dma((blocks,)),
                dma((n_exp, n_dp)),
                dma((blocks,)),
            ],
            compiler_params=pltpu.CompilerParams(
                collective_id=0, has_side_effects=True, vmem_limit_bytes=60 * 1024 * 1024
            ),
        )(tokens, ids.T, route.T, w_gate, w_up, w_down, past, dwa)

    return jax.shard_map(
        per_device,
        mesh=mesh,
        in_specs=(
            P(("expert", "dp"), None),
            P(("expert", "dp"), None),
            P(("expert", "dp"), None),
            P("expert", None, ("dp", "tensor")),
            P("expert", None, ("dp", "tensor")),
            P("expert", "dp", "tensor"),
            P(None, ("expert", "dp"), "tensor"),
            P(),
        ),
        out_specs=P(("expert", "dp"), "tensor"),
        check_vma=False,
    )
```
